32 devices in a mesh: wide: 16 (over z, y, x), narrow: 2 (over core).
Axes of the slice: x: 2, y: 2, z: 4, core: 2. Of those that a mesh axis runs over, the one named last changes fastest.
Arguments:
- amplitudes: bfloat16 [32768, 1024], P('wide', 'narrow'), may hold values from -6 to 6
- pair_mask: int32 [256, 8], P('wide', 'narrow'), may hold values 0 or 1
- integrals: bfloat16 [1024, 4096], P('wide', 'narrow'), may hold values from -0.1875 to 0.1875
Outputs:
- ladder: bfloat16 [32768, 4096], P('wide', 'narrow')
The draws below stay inside these ranges and needn't reach their ends.
All inputs are finite; a program needn't handle non-finite values. No bound on the sum of `pair_mask` on one device may be relied on, other than what follows from the above.
Results may differ from the reference program's by a relative error of at most 0.001.
Values may be sent and summed in bfloat16 or wider, within the bound.
No kernel may reach another device: no remote copies, remote signals or barrier semaphores. Data moves between devices by JAX's collectives and lax.ppermute only.
A program may use at most 64 MiB of HBM per device.

```python
import jax
import jax.numpy as jnp
from jax import lax

VB = 128
KBLK = 8
KV = 1024
PAIRS = 32768
NV = 4096
PBLK = 256


def with_ends(entries, rng, smallest, high):
    longest = entries.shape.index(max(entries.shape))
    spots = []
    for shift in (0, 1):
        where = [jax.random.randint(jax.random.fold_in(rng, axis), (), 0, length) for axis, length in enumerate(entries.shape)]
        where[longest] = (where[longest] + shift) % entries.shape[longest]
        spots.append(tuple(where))
    return entries.at[spots[0]].set(smallest).at[spots[1]].set(high)


def block_scale(stream_key, shape, pieces, low, top_value):
    factor_of = 1.0
    for axis_at, blocks in pieces:
        draws = jax.random.uniform(jax.random.fold_in(jax.random.fold_in(stream_key, 6), axis_at), (blocks,), jnp.float32, low / len(pieces), top_value / len(pieces))
        factor_of = factor_of * jnp.repeat(jnp.exp(draws), shape[axis_at] // blocks).reshape((-1,) + (1,) * (len(shape) - 1 - axis_at))
    return factor_of


def bell_draw(stream_key, shape, width, reach, split=(), dtype=jnp.bfloat16):
    loudness = block_scale(stream_key, shape, split, -0.22, 0.18) if split else 1.0
    entries = jax.random.normal(stream_key, shape, jnp.float32) * width * loudness
    return jnp.minimum(jnp.maximum(entries, -reach), reach).astype(dtype)


def setup_inputs(seed: int = 0) -> dict:
    splits = jax.random.split(jax.random.key(seed), 4)
    return {
        "amplitudes": bell_draw(splits[0], (PAIRS, KV), 1.0, 6.0, ((0, 16), (1, 2))),
        "pair_mask": with_ends((jax.random.randint(splits[1], (PBLK, KBLK), 0, 2) < 1).astype(jnp.int32), jax.random.fold_in(splits[1], 1), 0, 1),
        "integrals": bell_draw(splits[2], (KV, NV), KV ** -0.5, 0.1875, ((0, 16), (1, 2))),
    }


def reference(amplitudes, pair_mask, integrals):
    tiles = jnp.repeat(jnp.repeat(pair_mask, VB, axis=0), VB, axis=1)
    masked = amplitudes * tiles.astype(jnp.bfloat16)
    blocks = masked.reshape(PBLK, VB, KV)

    def one_block(rows):
        return jnp.dot(rows, integrals, preferred_element_type=jnp.float32).astype(jnp.bfloat16)

    out = lax.map(one_block, blocks)
    return out.reshape(PAIRS, NV)
```

```python
import functools

import jax
import jax.numpy as jnp
from jax import lax
from jax.experimental import pallas as pl
from jax.experimental.pallas import tpu as pltpu
from jax.sharding import PartitionSpec as P

AXES = ("wide", "narrow")


def exchange(value, sizes, flip):
    wide, narrow = sizes
    pairs = [
        (w * narrow + c, (w ^ flip(c)) * narrow + c)
        for w in range(wide)
        for c in range(narrow)
    ]
    return lax.ppermute(value, AXES, pairs)


def swap(value, sizes, flip):
    narrow = sizes[1]
    return lax.ppermute(value, "narrow", [(c, c ^ flip) for c in range(narrow)])


def product_kernel(rounds, last, parts, steps, tm, *refs):
    refs = list(refs)
    masks = [refs.pop(0) for _ in range(parts)]
    panels = [refs.pop(0) for _ in range(parts)]
    pieces = [[refs.pop(0) for _ in range(3)] for _ in rounds]
    before = refs.pop(0) if rounds[0] else None
    out_ref, a_buf, b_buf, sems = refs
    step = pl.program_id(0)
    w, c = lax.axis_index("wide"), lax.axis_index("narrow")
    depth = pieces[0][0].shape[0]
    chunk = 4 * depth
    across = panels[0].shape[1]
    per_part = across // chunk
    layer, place = w // 4, lax.rem(w, 4)
    first_flip = 1 + lax.rem(c, 2)

    @pl.when(step == 0)
    def _():
        for i, r in enumerate(rounds):
            at = layer ^ r
            owner = (at // per_part) ^ c
            column = pl.multiple_of(lax.rem(at, per_part) * chunk, chunk)
            for j in range(parts):
                @pl.when(owner == j)
                def _():
                    pltpu.make_async_copy(
                        panels[j].at[:, pl.ds(column, chunk)], a_buf.at[i], sems.at[i]
                    ).start()
        for i, r in enumerate(rounds):
            own, near, far = pieces[i]
            spots = (place, place ^ first_flip, place ^ (3 - first_flip), place ^ 3)
            blocks = (own[...], near[...], far[:depth], far[depth:])
            for spot, block in zip(spots, blocks):
                b_buf[pl.ds(pl.multiple_of(i * chunk + spot * depth, depth), depth)] = block
        for i, r in enumerate(rounds):
            pltpu.make_async_copy(a_buf.at[i], a_buf.at[i], sems.at[i]).wait()

    high = a_buf.shape[1] // masks[0].shape[0]
    broad = across // masks[0].shape[1]
    columns = []
    for i, r in enumerate(rounds):
        at = layer ^ r
        owner = (at // per_part) ^ c
        start = lax.rem(at, per_part) * (chunk // broad)
        for k in range(chunk // broad):
            tiles = []
            for m in range(tm // high):
                row, col = step * (tm // high) + m, start + k
                keep = masks[0][row, col]
                for j in range(1, parts):
                    keep = jnp.where(owner == j, masks[j][row, col], keep)
                tile = a_buf[i, pl.ds(pl.multiple_of(row * high, high), high), k * broad : (k + 1) * broad]
                tiles.append(tile * keep.astype(jnp.float32).astype(tile.dtype))
            columns.append(jnp.concatenate(tiles, axis=0))
    a = jnp.concatenate(columns, axis=1)
    total = jnp.dot(a, b_buf[...], preferred_element_type=jnp.float32)
    if before is not None:
        total += before[...]
    out_ref[...] = total.astype(out_ref.dtype)


def product(masks, panels, pieces, before, rounds, last, tm):
    rows, across = panels[0].shape
    depth, wide_cols = pieces[0][0].shape
    chunk = 4 * depth
    dtype = panels[0].dtype if last else jnp.float32
    whole = pl.BlockSpec(memory_space=pltpu.VMEM)
    flat = [x for three in pieces for x in three]
    tile = pl.BlockSpec((tm, wide_cols), lambda i: (i, 0))
    flops = 2 * rows * chunk * len(rounds) * wide_cols
    return pl.pallas_call(
        functools.partial(product_kernel, rounds, last, len(panels), rows // tm, tm),
        out_shape=jax.ShapeDtypeStruct((rows, wide_cols), dtype),
        grid=(rows // tm,),
        in_specs=[pl.BlockSpec(memory_space=pltpu.SMEM)] * len(masks)
        + [pl.BlockSpec(memory_space=pl.ANY)] * len(panels)
        + [whole] * len(flat)
        + [tile] * (before is not None),
        out_specs=tile,
        scratch_shapes=[
            pltpu.VMEM((len(rounds), rows, chunk), panels[0].dtype),
            pltpu.VMEM((len(rounds) * chunk, wide_cols), panels[0].dtype),
            pltpu.SemaphoreType.DMA((len(rounds),)),
        ],
        compiler_params=pltpu.CompilerParams(vmem_limit_bytes=32 * 2**20),
        cost_estimate=pl.CostEstimate(
            flops=flops, bytes_accessed=flops // 2048, transcendentals=0
        ),
        name="product" + "".join(map(str, rounds)),
    )(*masks, *panels, *flat, *([] if before is None else [before]))


def shards(sizes, amplitudes, pair_mask, integrals):
    wide, narrow = sizes
    first = lambda c: 1 + c % 2
    second = lambda c: 2 - c % 2
    layers = wide // 4
    masks = [pair_mask] + [swap(pair_mask, sizes, j) for j in range(1, narrow)]
    panels = [amplitudes] + [swap(amplitudes, sizes, j) for j in range(1, narrow)]
    own = {0: integrals}
    for r in range(1, layers):
        own[r] = exchange(integrals, sizes, lambda c: 4 * r)
    pieces = {}
    for r in range(layers):
        if r == 1:
            near = exchange(pieces[0][1], sizes, lambda c: 4)
        else:
            near = exchange(own[r], sizes, first)
        far = exchange(jnp.concatenate([own[r], near], axis=0), sizes, second)
        pieces[r] = (own[r], near, far)
    groups = [range(0, layers // 2), range(layers // 2, layers - 1), range(layers - 1, layers)]
    total = None
    for rounds in groups:
        rounds = list(rounds)
        total = product(
            masks, panels, [pieces[r] for r in rounds], total, rounds, rounds[-1] == layers - 1, 256
        )
    return total


def solution(mesh):
    sizes = (mesh.shape["wide"], mesh.shape["narrow"])
    specs = P("wide", "narrow")
    return jax.shard_map(
        functools.partial(shards, sizes), mesh=mesh, in_specs=(specs,) * 3, out_specs=specs, check_vma=False
    )
```

```python
import functools

import jax
import jax.numpy as jnp
from jax import lax
from jax.experimental import pallas as pl
from jax.experimental.pallas import tpu as pltpu
from jax.sharding import PartitionSpec as P


AXES = ("wide", "narrow")
TILE = 512
SPANS = 4


def placed(round_, chunk, per_part):
    at = (lax.axis_index("wide") // 4) ^ round_
    owner = (at // per_part) ^ lax.axis_index("narrow")
    return owner, lax.rem(at, per_part) * chunk


def panel_kernel(rounds, chunk, parts, *refs):
    masks, panels = refs[:parts], refs[parts : 2 * parts]
    out_ref, held, sems = refs[2 * parts :]
    rows, across = panels[0].shape
    high = rows // masks[0].shape[1]
    broad = across // masks[0].shape[0]
    span = rows // sems.shape[1]

    def copy(j, s):
        at = pl.ds(s * span, span)
        return pltpu.make_async_copy(panels[j].at[at], held.at[j, at], sems.at[j, s])

    for s in range(sems.shape[1]):
        for j in range(parts):
            copy(j, s).start()
    for s in range(sems.shape[1]):
        for j in range(parts):
            copy(j, s).wait()
        for r in range(rounds):
            owner, column = placed(r, chunk, across // chunk)
            for j in range(parts):

                @pl.when(owner == j)
                def _():
                    for m in range(span // high):
                        row = s * (span // high) + m
                        for k in range(chunk // broad):
                            keep = masks[j][column // broad + k, row]
                            start = pl.multiple_of(column + k * broad, broad)
                            tile = held[j, row * high : (row + 1) * high, pl.ds(start, broad)]
                            out_ref[
                                r, row * high : (row + 1) * high, k * broad : (k + 1) * broad
                            ] = tile * keep.astype(jnp.float32).astype(tile.dtype)


def make_panel(masks, panels, rounds, chunk):
    rows, across = panels[0].shape
    parts = len(panels)
    moved = parts * rows * across * 2
    return pl.pallas_call(
        functools.partial(panel_kernel, rounds, chunk, parts),
        out_shape=jax.ShapeDtypeStruct((rounds, rows, chunk), panels[0].dtype),
        in_specs=[pl.BlockSpec(memory_space=pltpu.SMEM)] * parts
        + [pl.BlockSpec(memory_space=pltpu.HBM)] * parts,
        out_specs=pl.BlockSpec(memory_space=pltpu.VMEM),
        scratch_shapes=[
            pltpu.VMEM((parts, rows, across), panels[0].dtype),
            pltpu.SemaphoreType.DMA((parts, SPANS)),
        ],
        compiler_params=pltpu.CompilerParams(vmem_limit_bytes=12 * 2**20),
        cost_estimate=pl.CostEstimate(flops=0, bytes_accessed=moved, transcendentals=0),
        name="panel",
    )(*masks, pltpu.with_memory_space_constraint(panels[0], pltpu.HBM), *panels[1:])


def product_kernel(rounds, first, last, *refs):
    refs = list(refs)
    panel = refs.pop(0)
    pieces = [[refs.pop(0) for _ in range(4)] for _ in rounds]
    before = None if first else refs.pop(0)
    out_ref, b_buf = refs
    depth = pieces[0][0].shape[0]
    chunk = 4 * depth

    @pl.when(pl.program_id(0) == 0)
    def _():
        place = lax.rem(lax.axis_index("wide"), 4)
        flip = 1 + lax.rem(lax.axis_index("narrow"), 2)
        spots = (place, place ^ flip, place ^ (3 - flip), place ^ 3)
        for i in range(len(rounds)):
            for spot, piece in zip(spots, pieces[i]):
                at = pl.multiple_of(i * chunk + spot * depth, depth)
                b_buf[pl.ds(at, depth)] = piece[...]

    at = pl.ds(pl.multiple_of(pl.program_id(0) * TILE, TILE), TILE)
    a = jnp.concatenate([panel[r, at] for r in rounds], axis=1)
    for n in range(0, b_buf.shape[1], 256):
        total = jnp.dot(a, b_buf[:, n : n + 256], preferred_element_type=jnp.float32)
        if before is not None:
            total += before[at, n : n + 256]
        if last:
            out_ref[:, n : n + 256] = total.astype(out_ref.dtype)
        else:
            out_ref[at, n : n + 256] = total


def product(panel, pieces, before, rounds, last):
    _, rows, chunk = panel.shape
    columns = pieces[0][0].shape[1]
    whole = pl.BlockSpec(memory_space=pltpu.VMEM)
    flat = [x for four in pieces for x in four]
    flops = 2 * rows * chunk * len(rounds) * columns
    first = before is None
    return pl.pallas_call(
        functools.partial(product_kernel, rounds, first, last),
        out_shape=jax.ShapeDtypeStruct(
            (rows, columns), panel.dtype if last else jnp.float32
        ),
        grid=(rows // TILE,),
        in_specs=[whole] * (1 + len(flat) + (not first)),
        out_specs=pl.BlockSpec((TILE, columns), lambda i: (i, 0)) if last else whole,
        scratch_shapes=[pltpu.VMEM((len(rounds) * chunk, columns), panel.dtype)],
        input_output_aliases={} if first or last else {1 + len(flat): 0},
        compiler_params=pltpu.CompilerParams(vmem_limit_bytes=16 * 2**20),
        cost_estimate=pl.CostEstimate(
            flops=flops, bytes_accessed=rows * columns * 2, transcendentals=0
        ),
    )(panel, *flat, *([] if first else [before]))


def shards(sizes, amplitudes, pair_mask, integrals):
    wide, narrow = sizes
    layers = wide // 4

    def exchange(value, flip):
        pairs = [
            (w * narrow + c, (w ^ flip(c)) * narrow + c)
            for w in range(wide)
            for c in range(narrow)
        ]
        return lax.ppermute(value, AXES, pairs)

    def swap(value, flip):
        return lax.ppermute(value, "narrow", [(c, c ^ flip) for c in range(narrow)])

    panels = [amplitudes] + [swap(amplitudes, j) for j in range(1, narrow)]
    turned = pair_mask.T
    masks = [turned] + [swap(turned, j) for j in range(1, narrow)]
    panel = make_panel(masks, panels, layers, 4 * integrals.shape[0])
    total = None
    for r in range(layers):
        own = exchange(integrals, lambda c: 4 * r) if r else integrals
        near = exchange(own, lambda c: 1 + c % 2)
        side = exchange(own, lambda c: 2 - c % 2)
        far = exchange(near, lambda c: 2 - c % 2)
        total = product(panel, [(own, near, side, far)], total, [r], r == layers - 1)
    return total


def solution(mesh):
    sizes = (mesh.shape["wide"], mesh.shape["narrow"])
    specs = P("wide", "narrow")
    return jax.shard_map(
        functools.partial(shards, sizes), mesh=mesh, in_specs=(specs,) * 3, out_specs=specs, check_vma=False
    )
```
